256 devices in a mesh: dp: 8 (over z), expert: 32 (over y, x, core).
Axes of the slice: x: 4, y: 4, z: 8, core: 2. Of those that a mesh axis runs over, the one named last changes fastest.
Arguments:
- x_routed: bfloat16 [32, 1024, 2048], P(None, 'dp', 'expert'), may hold values from -10 to 10
- grad_out: bfloat16 [32, 1024, 768], P(None, 'dp'), may hold values from -15 to 15
- block_counts: int32 [8, 32], P('dp'), may hold values from 1 to 8, as said below
Outputs:
- update: bfloat16 [32, 2048, 768], P(None, 'expert')
The draws below stay inside these ranges and needn't reach their ends.
Inputs may be any that keep to these rules, and one draw needn't show every extreme that they name: Rows of replica r beyond 16 * block_counts[r, e] of expert e are padding; on every replica one expert has all 128 rows live.
All inputs are finite; a program needn't handle non-finite values.
Results may differ from the reference program's by a relative error of at most 0.0065.
Values may be sent and summed in bfloat16 or wider, within the bound.
No kernel may reach another device: no remote copies, remote signals or barrier semaphores. Data moves between devices by JAX's collectives and lax.ppermute only.
A program may use at most 64 MiB of HBM per device.

```python
import math
import jax
import jax.numpy as jnp
from jax import lax

D = 2048
FF = 768
CAP = 128
BLK = 16
ITERS = 2
EXPERTS = 32
REPLICAS = 8


def column_scales(key_cols, number):
    return jnp.exp(jax.random.uniform(key_cols, (number,), jnp.float32, 0.0, math.log(10.0)))


def draw_x_routed(key, part):
    key_base, key_cols = jax.random.split(jax.random.fold_in(key, 11), 2)
    array_shape = (EXPERTS, CAP * REPLICAS, D)
    values_base = jnp.clip(jax.random.normal(key_base, array_shape, jnp.float32), -4.0, 4.0)
    return (values_base * column_scales(key_cols, D)[None, None, :] / 4.0).astype(jnp.bfloat16)


def draw_grad_out(key, part):
    key_base, key_cols = jax.random.split(jax.random.fold_in(key, 23), 2)
    array_shape = (EXPERTS, CAP * REPLICAS, FF)
    replica = (jnp.arange(CAP * REPLICAS) // CAP).astype(jnp.float32)
    rising = 1.0 + 2.0 * replica / max(REPLICAS - 1, 1)
    values_base = jnp.clip(jax.random.normal(key_base, array_shape, jnp.float32), -4.0, 4.0)
    scaled = values_base * rising[None, :, None] * column_scales(key_cols, FF)[None, None, :] / 10.0
    return scaled.astype(jnp.bfloat16)


def draw_block_counts(key, part):
    key_values, key_full = jax.random.split(jax.random.fold_in(key, 37))
    blocks = CAP // BLK
    values_drawn = jax.random.randint(key_values, (REPLICAS, EXPERTS), 1, blocks + 1)
    full_expert = jax.random.randint(key_full, (REPLICAS, 1), 0, EXPERTS)
    expert_index = jnp.arange(EXPERTS)[None, :]
    return jnp.where(expert_index == full_expert, blocks, values_drawn).astype(jnp.int32)


def setup_inputs(seed: int = 0) -> dict:
    keys = jax.random.split(jax.random.key(seed), 4)
    return {
        "x_routed": draw_x_routed(jax.random.fold_in(keys[3], 71), 0),
        "grad_out": draw_grad_out(jax.random.fold_in(keys[3], 71), 0),
        "block_counts": draw_block_counts(jax.random.fold_in(keys[3], 71), 0),
    }


NEWTON_FIRST = 3.4445
NEWTON_SECOND = -4.775
NEWTON_THIRD = 2.0315
EPSILON = 1e-07

def live_rows(block_counts):
    row_index = jnp.arange(CAP * REPLICAS, dtype=jnp.int32)
    within = row_index % CAP
    replica = row_index // CAP
    limit = BLK * block_counts.T[:, replica]
    return within[None, :] < limit

def orthogonal(gradient):
    total = jnp.sum(gradient * gradient)
    current = (gradient / (jnp.sqrt(total) + EPSILON)).astype(jnp.bfloat16)
    for iteration in range(ITERS):
        gram_matrix = lax.dot_general(current, current, (((0,), (0,)), ((), ())), preferred_element_type=jnp.float32).astype(jnp.bfloat16)
        square = jnp.dot(gram_matrix, gram_matrix, preferred_element_type=jnp.float32)
        polynomial = (NEWTON_SECOND * gram_matrix.astype(jnp.float32) + NEWTON_THIRD * square).astype(jnp.bfloat16)
        combined = NEWTON_FIRST * current.astype(jnp.float32) + jnp.dot(current, polynomial, preferred_element_type=jnp.float32)
        if iteration + 1 == ITERS:
            combined = combined * math.sqrt(D)
        current = combined.astype(jnp.bfloat16)
    return current

def one_expert(operands):
    x_expert, grad_expert = operands
    gradient = lax.dot_general(x_expert, grad_expert, (((0,), (0,)), ((), ())), preferred_element_type=jnp.float32)
    return orthogonal(gradient)

def reference(x_routed, grad_out, block_counts):
    live_mask = live_rows(block_counts)
    masked = jnp.where(live_mask[:, :, None], grad_out, jnp.zeros((), grad_out.dtype))
    return lax.map(one_expert, (x_routed, masked))
```

```python
import math

import jax
import jax.numpy as jnp
from jax import lax
from jax.experimental import pallas as pl
from jax.experimental.pallas import tpu as pltpu
from jax.sharding import Mesh, PartitionSpec as P

BLK = 16
NEWTON_FIRST = 3.4445
NEWTON_SECOND = -4.775
NEWTON_THIRD = 2.0315
EPSILON = 1e-07


NZ, NY, NX, NC = 8, 4, 4, 2


def shift(n, k):
    return [(i, (i + k) % n) for i in range(n)]


def dot(a, b):
    return jnp.dot(a, b, preferred_element_type=jnp.float32)


def grad_kernel(place, xt_ref, *refs):
    pieces, out_ref, rows = refs[:-2], refs[-2], refs[-1]
    half = NZ // 2
    for core in range(2):
        own, right, left, far_a, far_b = pieces[5 * core : 5 * core + 5]
        for offset, ref, first in (
            (0, own, 0),
            (1, right, 0),
            (2, left, 0),
            (3, far_a, 0),
            (3, far_b, half),
        ):
            block = place[4 * core + offset]
            for r in range(ref.shape[0]):
                rows[first + r, block] = ref[r]
    total = None
    for r in range(0, NZ, 2):
        left = jnp.concatenate(
            [xt_ref[:, r].reshape(256, 128), xt_ref[:, r + 1].reshape(256, 128)], axis=1
        )
        right = rows[r : r + 2].reshape(256, rows.shape[-1])
        part = dot(left, right)
        total = part if total is None else total + part
    out_ref[...] = total.astype(jnp.bfloat16)


def newton_kernel(scale, mine_ref, other_ref, grad_ref, out_ref):
    raw = mine_ref[...] + other_ref[...]
    n = raw.shape[0]
    diagonal = lax.broadcasted_iota(jnp.int32, (n, n), 0) == lax.broadcasted_iota(
        jnp.int32, (n, n), 1
    )
    norm = jnp.sqrt(jnp.sum(jnp.where(diagonal, raw, 0.0), keepdims=True))
    inverse = 1.0 / (norm + EPSILON)
    gram = raw * inverse * inverse
    gram16 = gram.astype(jnp.bfloat16)
    first = (NEWTON_SECOND * gram + NEWTON_THIRD * dot(gram16, gram16)).astype(jnp.bfloat16)
    grad = grad_ref[...]
    current = inverse * (NEWTON_FIRST * grad.astype(jnp.float32) + dot(grad, first))
    half = NEWTON_FIRST * gram + dot(first, gram16)
    gram = NEWTON_FIRST * half + dot(half.astype(jnp.bfloat16), first)
    gram16 = gram.astype(jnp.bfloat16)
    second = (NEWTON_SECOND * gram + NEWTON_THIRD * dot(gram16, gram16)).astype(jnp.bfloat16)
    out = NEWTON_FIRST * current + dot(current.astype(jnp.bfloat16), second)
    out_ref[...] = (scale * out).astype(jnp.bfloat16)


def gram_of(rows):
    return lax.dot_general(rows, rows, (((0,), (0,)), ((), ())), preferred_element_type=jnp.float32)


def per_device(x, g, counts):
    width = g.shape[2]
    zi, yi, xi, ci = (lax.axis_index(a) for a in "zyxc")
    block = 2 * xi + ci

    g5 = g.reshape(NZ, NY, 8, BLK, width)
    mine = lax.dynamic_slice(g5, (0, yi, block, 0, 0), (NZ, 1, 1, BLK, width))
    mine = mine.reshape(NZ, BLK, width)
    count = lax.dynamic_slice(counts.reshape(NZ, NY), (0, yi), (NZ, 1))[:, :, None]
    mine = jnp.where(block < count, mine, jnp.zeros((), mine.dtype))
    own = lax.all_to_all(mine, "z", 0, 0, tiled=True)

    right = lax.ppermute(own, "x", shift(NX, 1))
    left = lax.ppermute(own, "x", shift(NX, -1))
    far_a = lax.ppermute(right[: NZ // 2], "x", shift(NX, 1))
    far_b = lax.ppermute(left[NZ // 2 :], "x", shift(NX, -1))
    pieces = [own, right, left, far_a, far_b]
    pieces = pieces + [lax.ppermute(p, "c", shift(NC, 1)) for p in pieces]

    xt = x.transpose(0, 2, 1).reshape(NZ, NY, 64, 128)
    xz = lax.all_to_all(xt, "z", 0, 0, tiled=True)
    xy = lax.all_to_all(xz.transpose(1, 0, 2, 3), "y", 0, 0, tiled=True)

    xs = jnp.stack([xi, (xi + NX - 1) % NX, (xi + 1) % NX, (xi + 2) % NX])
    place = jnp.concatenate([2 * xs + ci, 2 * xs + 1 - ci]).astype(jnp.int32)
    vmem = pl.BlockSpec(memory_space=pltpu.VMEM)
    grad = pl.pallas_call(
        grad_kernel,
        out_shape=jax.ShapeDtypeStruct((256, width), jnp.bfloat16),
        in_specs=[pl.BlockSpec(memory_space=pltpu.SMEM)] + [vmem] * 11,
        out_specs=vmem,
        scratch_shapes=[pltpu.VMEM((NZ, 8, BLK, width), jnp.bfloat16)],
        name="grad",
    )(place, xy, *pieces)

    right = lax.ppermute(grad, "x", shift(NX, 1))
    left = lax.ppermute(grad, "x", shift(NX, -1))
    far_a = lax.ppermute(right[:128], "x", shift(NX, 1))
    far_b = lax.ppermute(left[128:], "x", shift(NX, -1))
    total = gram_of(grad) + gram_of(right) + gram_of(left) + gram_of(far_a) + gram_of(far_b)
    other = lax.ppermute(total, "c", shift(NC, 1))

    rows = pl.pallas_call(
        lambda *refs: newton_kernel(math.sqrt(2048), *refs),
        out_shape=jax.ShapeDtypeStruct((256, width), jnp.bfloat16),
        in_specs=[vmem] * 3,
        out_specs=vmem,
        name="newton",
    )(total, other, grad)

    mine = lax.all_to_all(rows.reshape(NY, 64, width), "y", 0, 0, tiled=True)
    out = jnp.zeros((NZ, NY, 64, width), jnp.bfloat16)

    def put(out, piece, plane, at=0):
        return lax.dynamic_update_slice(out, piece[None], (plane % NZ, at, 0, 0))

    out = put(out, mine, zi)
    right, left = mine, mine
    for step in range(1, 4):
        right = lax.ppermute(right, "z", shift(NZ, 1))
        left = lax.ppermute(left, "z", shift(NZ, -1))
        out = put(out, right, zi + NZ - step)
        out = put(out, left, zi + step)
    far_a = lax.ppermute(right[:2], "z", shift(NZ, 1))
    far_b = lax.ppermute(left[2:], "z", shift(NZ, -1))
    out = put(out, far_a, zi + 4)
    out = put(out, far_b, zi + 4, 2)
    return out.reshape(NZ * NY, 64, width)


def solution(mesh):
    fine = Mesh(mesh.devices.reshape(NZ, NY, NX, NC), ("z", "y", "x", "c"))
    return jax.shard_map(
        per_device,
        mesh=fine,
        in_specs=(P(None, "z", ("y", "x", "c")), P(None, "z", None), P("z", None)),
        out_specs=P(None, ("y", "x", "c"), None),
        check_vma=False,
    )
```

```python
import functools
import math

import jax
import jax.numpy as jnp
from jax import lax
from jax.experimental import pallas as pl
from jax.experimental.pallas import tpu as pltpu
from jax.sharding import Mesh, PartitionSpec as P

BLK = 16
NEWTON_FIRST = 3.4445
NEWTON_SECOND = -4.775
NEWTON_THIRD = 2.0315
EPSILON = 1e-07


NZ, NY, NX, NC = 8, 4, 4, 2
COLS, CAP = 64, 128

VMEM = pl.BlockSpec(memory_space=pltpu.VMEM)
SMEM = pl.BlockSpec(memory_space=pltpu.SMEM)
ANY = pl.BlockSpec(memory_space=pl.ANY)


def shift(n, k):
    return [(i, (i + k) % n) for i in range(n)]


def near(*arrays):
    return [pltpu.with_memory_space_constraint(a, pltpu.VMEM) for a in arrays]


def dot(a, b):
    return jnp.dot(a, b, preferred_element_type=jnp.float32)


def gram_of(rows):
    return lax.dot_general(rows, rows, (((0,), (0,)), ((), ())), preferred_element_type=jnp.float32)


def pack_kernel(count_ref, g_ref, out_ref, sem):
    y = lax.axis_index("y")
    block = NC * lax.axis_index("x") + lax.axis_index("c")
    copy = pltpu.make_async_copy(g_ref.at[y, :, block], out_ref, sem)
    copy.start()
    copy.wait()
    for plane in range(NZ):

        @pl.when(block >= count_ref[0, NZ * y + plane])
        def _():
            out_ref[plane] = jnp.zeros(out_ref.shape[1:], out_ref.dtype)


def grad_kernel(xt_ref, *refs):
    pieces, out_ref, rows = refs[:-2], refs[-2], refs[-1]
    x, c = lax.axis_index("x"), lax.axis_index("c")
    half = NZ // 2
    for core in range(NC):
        own, right, left, far_a, far_b = pieces[5 * core : 5 * core + 5]
        for offset, ref, first in (
            (0, own, 0),
            (3, right, 0),
            (1, left, 0),
            (2, far_a, 0),
            (2, far_b, half),
        ):
            block = NC * lax.rem(x + offset, NX) + (c if core == 0 else 1 - c)
            for r in range(ref.shape[0]):
                rows[first + r, block] = ref[r]
    total = None
    for r in range(0, NZ, 2):
        lhs = jnp.concatenate(
            [xt_ref[r].reshape(NY * COLS, CAP), xt_ref[r + 1].reshape(NY * COLS, CAP)], axis=1
        )
        part = dot(lhs, rows[r : r + 2].reshape(2 * CAP, rows.shape[-1]))
        total = part if total is None else total + part
    out_ref[...] = total.astype(jnp.bfloat16)


def newton_kernel(scale, mine_ref, other_ref, far_a_ref, far_b_ref, grad_ref, *out_refs):
    far = jnp.concatenate([far_a_ref[...], far_b_ref[...]], axis=0)
    raw = mine_ref[...] + other_ref[...] + gram_of(far)
    n = raw.shape[0]
    diagonal = lax.broadcasted_iota(jnp.int32, (n, n), 0) == lax.broadcasted_iota(
        jnp.int32, (n, n), 1
    )
    norm = jnp.sqrt(jnp.sum(jnp.where(diagonal, raw, 0.0), keepdims=True))
    inverse = 1.0 / (norm + EPSILON)
    gram = raw * inverse * inverse
    gram16 = gram.astype(jnp.bfloat16)
    first = (NEWTON_SECOND * gram + NEWTON_THIRD * dot(gram16, gram16)).astype(jnp.bfloat16)
    y = lax.axis_index("y")
    grad = jnp.concatenate(
        [
            grad_ref[pl.ds(pl.multiple_of(COLS * lax.rem(y + k, NY), COLS), COLS), :]
            for k in range(NY)
        ],
        axis=0,
    )
    current = inverse * (NEWTON_FIRST * grad.astype(jnp.float32) + dot(grad, first))
    half = NEWTON_FIRST * gram + dot(first, gram16)
    gram = NEWTON_FIRST * half + dot(half.astype(jnp.bfloat16), first)
    gram16 = gram.astype(jnp.bfloat16)
    second = (NEWTON_SECOND * gram + NEWTON_THIRD * dot(gram16, gram16)).astype(jnp.bfloat16)
    out = NEWTON_FIRST * current + dot(current.astype(jnp.bfloat16), second)
    out = (scale * out).astype(jnp.bfloat16)
    for k in range(NY):
        out_refs[k][...] = out[COLS * k : COLS * (k + 1)]


def place_kernel(places, n, aliased, *refs):
    pieces, (out_ref, sems) = refs[:n], refs[n + aliased :]
    y, z = lax.axis_index("y"), lax.axis_index("z")
    copies = []
    for piece, (dys, dz, row) in zip(pieces, places):
        for index, dy in enumerate(dys):
            target = out_ref.at[
                lax.rem(y + dy, NY), lax.rem(z + dz + NZ, NZ), pl.ds(row, piece.shape[1])
            ]
            copies.append(pltpu.make_async_copy(piece.at[index], target, sems.at[len(copies)]))
            copies[-1].start()
    for copy in copies:
        copy.wait()


def place(out, width, items, name):
    pieces = near(*(piece for piece, _ in items))
    places = [where for _, where in items]
    n = len(pieces)
    aliased = out is not None
    return pl.pallas_call(
        functools.partial(place_kernel, places, n, int(aliased)),
        out_shape=jax.ShapeDtypeStruct((NY, NZ, COLS, width), jnp.bfloat16),
        in_specs=[VMEM] * n + [ANY] * aliased,
        out_specs=ANY,
        scratch_shapes=[pltpu.SemaphoreType.DMA((sum(len(w[0]) for w in places),))],
        input_output_aliases={n: 0} if aliased else {},
        compiler_params=pltpu.CompilerParams(vmem_limit_bytes=4 << 20),
        name=name,
    )(*pieces, *([out] if aliased else []))


def per_device(x, g, counts):
    width = g.shape[2]

    xt = x.transpose(0, 2, 1).reshape(NY, NZ, COLS, CAP)
    xy = lax.all_to_all(xt, "y", 0, 0, tiled=True)
    xz = lax.all_to_all(xy.transpose(1, 0, 2, 3), "z", 0, 0, tiled=True)

    blocks = g.reshape(NY, NZ, CAP // BLK, BLK, width)
    mine = pl.pallas_call(
        pack_kernel,
        out_shape=pltpu.VMEM((NZ, BLK, width), jnp.bfloat16),
        in_specs=[SMEM, ANY],
        out_specs=VMEM,
        scratch_shapes=[pltpu.SemaphoreType.DMA],
        compiler_params=pltpu.CompilerParams(vmem_limit_bytes=2 << 20),
        name="pack",
    )(counts, pltpu.with_memory_space_constraint(blocks, pltpu.HBM))
    own = lax.all_to_all(mine, "z", 0, 0, tiled=True)
    right = lax.ppermute(own, "x", shift(NX, 1))
    left = lax.ppermute(own, "x", shift(NX, -1))
    far_a = lax.ppermute(right[: NZ // 2], "x", shift(NX, 1))
    far_b = lax.ppermute(left[NZ // 2 :], "x", shift(NX, -1))
    pieces = [own, right, left, far_a, far_b]
    pieces = pieces + [lax.ppermute(p, "c", shift(NC, 1)) for p in pieces]

    grad = pl.pallas_call(
        grad_kernel,
        out_shape=pltpu.VMEM((NY * COLS, width), jnp.bfloat16),
        in_specs=[VMEM] * 11,
        out_specs=VMEM,
        scratch_shapes=[pltpu.VMEM((NZ, CAP // BLK, BLK, width), jnp.bfloat16)],
        compiler_params=pltpu.CompilerParams(vmem_limit_bytes=12 << 20),
        name="grad",
    )(*near(xz, *pieces))

    mid = NY * COLS // 2
    right_a = lax.ppermute(grad[:mid], "x", shift(NX, 1))
    left_b = lax.ppermute(grad[mid:], "x", shift(NX, -1))
    right_b = lax.ppermute(grad[mid:], "x", shift(NX, 1))
    left_a = lax.ppermute(grad[:mid], "x", shift(NX, -1))
    far_a = lax.ppermute(right_a, "x", shift(NX, 1))
    far_b = lax.ppermute(left_b, "x", shift(NX, -1))
    total = gram_of(grad)
    for part in (right_a, left_b, right_b, left_a):
        total = total + gram_of(part)
    other = lax.ppermute(total, "c", shift(NC, 1))
    other_far_a = lax.ppermute(far_a, "c", shift(NC, 1))
    other_far_b = lax.ppermute(far_b, "c", shift(NC, 1))
    total = total + gram_of(far_a) + gram_of(far_b)

    own, ahead, across, behind = pl.pallas_call(
        functools.partial(newton_kernel, math.sqrt(2048)),
        out_shape=[pltpu.VMEM((COLS, width), jnp.bfloat16)] * NY,
        in_specs=[VMEM] * 5,
        out_specs=[VMEM] * NY,
        compiler_params=pltpu.CompilerParams(vmem_limit_bytes=32 << 20),
        name="newton",
    )(*near(total, other, other_far_a, other_far_b, grad))

    moved = jnp.stack(
        [
            lax.ppermute(ahead, "y", shift(NY, 1)),
            lax.ppermute(behind, "y", shift(NY, -1)),
            lax.ppermute(across, "y", shift(NY, 2)),
        ]
    )
    streams = [(own[None], (0,)), (moved, (3, 1, 2))]
    rings = []
    for start, dys in streams:
        right, left = start, start
        ring = [(start, (dys, 0, 0))]
        for step in range(1, 4):
            right = lax.ppermute(right, "z", shift(NZ, 1))
            left = lax.ppermute(left, "z", shift(NZ, -1))
            ring += [(right, (dys, -step, 0)), (left, (dys, step, 0))]
        half = COLS // 2
        ring.append((lax.ppermute(right[:, :half], "z", shift(NZ, 1)), (dys, 4, 0)))
        ring.append((lax.ppermute(left[:, half:], "z", shift(NZ, -1)), (dys, 4, half)))
        rings.append(ring)
    out = place(None, width, rings[0] + rings[1][:3], "place_0")
    out = place(out, width, rings[1][3:7], "place_1")
    out = place(out, width, rings[1][7:], "place_2")
    return out.reshape(NY * NZ, COLS, width)


def solution(mesh):
    fine = Mesh(mesh.devices.reshape(NZ, NY, NX, NC), ("z", "y", "x", "c"))
    return jax.shard_map(
        per_device,
        mesh=fine,
        in_specs=(P(None, "z", ("y", "x", "c")), P(None, "z", None), P("z", None)),
        out_specs=P(None, ("y", "x", "c"), None),
        check_vma=False,
    )
```

```python
import functools
import math

import jax
import jax.numpy as jnp
from jax import lax
from jax.experimental import pallas as pl
from jax.experimental.pallas import tpu as pltpu
from jax.sharding import Mesh, PartitionSpec as P

BLK = 16
NEWTON_FIRST = 3.4445
NEWTON_SECOND = -4.775
NEWTON_THIRD = 2.0315
EPSILON = 1e-07


NZ, NY, NX, NC = 8, 4, 4, 2
COLS, CAP = 64, 128
SIDES = (0, 1, 3, 2)

VMEM = pl.BlockSpec(memory_space=pltpu.VMEM)
SMEM = pl.BlockSpec(memory_space=pltpu.SMEM)
ANY = pl.BlockSpec(memory_space=pl.ANY)


def shift(n, k):
    return [(i, (i + k) % n) for i in range(n)]


def near(*arrays):
    return [pltpu.with_memory_space_constraint(a, pltpu.VMEM) for a in arrays]


def dot(a, b):
    return jnp.dot(a, b, preferred_element_type=jnp.float32)


def gram_of(rows):
    return lax.dot_general(rows, rows, (((0,), (0,)), ((), ())), preferred_element_type=jnp.float32)


def pack_kernel(count_ref, x_ref, g_ref, *refs):
    x_outs, g_out, sems = refs[:NY], refs[NY], refs[NY + 1]
    y = lax.axis_index("y")
    block = NC * lax.axis_index("x") + lax.axis_index("c")
    copies = [pltpu.make_async_copy(g_ref.at[y, :, block], g_out, sems.at[NY])]
    for k, dy in enumerate(SIDES):
        source = x_ref.at[lax.rem(y + dy, NY)]
        copies.append(pltpu.make_async_copy(source, x_outs[k], sems.at[k]))
    for copy in copies:
        copy.start()
    for copy in copies:
        copy.wait()
    for plane in range(NZ):

        @pl.when(block >= count_ref[0, NZ * y + plane])
        def _():
            g_out[plane] = jnp.zeros(g_out.shape[1:], g_out.dtype)


def grad_kernel(xt_ref, *refs):
    pieces, out_ref, rows = refs[:-2], refs[-2], refs[-1]
    x, c = lax.axis_index("x"), lax.axis_index("c")
    half = NZ // 2
    for core in range(NC):
        own, right, left, far_a, far_b = pieces[5 * core : 5 * core + 5]
        for offset, ref, first in (
            (0, own, 0),
            (3, right, 0),
            (1, left, 0),
            (2, far_a, 0),
            (2, far_b, half),
        ):
            block = NC * lax.rem(x + offset, NX) + (c if core == 0 else 1 - c)
            for r in range(ref.shape[0]):
                rows[first + r, block] = ref[r]
    total = None
    for r in range(0, NZ, 2):
        lhs = jnp.concatenate(
            [xt_ref[r].reshape(NY * COLS, CAP), xt_ref[r + 1].reshape(NY * COLS, CAP)], axis=1
        )
        part = dot(lhs, rows[r : r + 2].reshape(2 * CAP, rows.shape[-1]))
        total = part if total is None else total + part
    out_ref[...] = total.astype(jnp.bfloat16)


def newton_kernel(scale, mine_ref, other_ref, far_a_ref, far_b_ref, grad_ref, *out_refs):
    far = jnp.concatenate([far_a_ref[...], far_b_ref[...]], axis=0)
    raw = mine_ref[...] + other_ref[...] + gram_of(far)
    n = raw.shape[0]
    diagonal = lax.broadcasted_iota(jnp.int32, (n, n), 0) == lax.broadcasted_iota(
        jnp.int32, (n, n), 1
    )
    norm = jnp.sqrt(jnp.sum(jnp.where(diagonal, raw, 0.0), keepdims=True))
    inverse = 1.0 / (norm + EPSILON)
    gram = raw * inverse * inverse
    gram16 = gram.astype(jnp.bfloat16)
    first = (NEWTON_SECOND * gram + NEWTON_THIRD * dot(gram16, gram16)).astype(jnp.bfloat16)
    grad = grad_ref[...]
    current = inverse * (NEWTON_FIRST * grad.astype(jnp.float32) + dot(grad, first))
    half = NEWTON_FIRST * gram + dot(first, gram16)
    gram = NEWTON_FIRST * half + dot(half.astype(jnp.bfloat16), first)
    gram16 = gram.astype(jnp.bfloat16)
    second = (NEWTON_SECOND * gram + NEWTON_THIRD * dot(gram16, gram16)).astype(jnp.bfloat16)
    out = NEWTON_FIRST * current + dot(current.astype(jnp.bfloat16), second)
    out = (scale * out).astype(jnp.bfloat16)
    for k in range(NY):
        out_refs[k][...] = out[COLS * k : COLS * (k + 1)].reshape(out_refs[k].shape)


def place_kernel(places, n, aliased, *refs):
    pieces, (out_ref, sems) = refs[:n], refs[n + aliased :]
    y, z = lax.axis_index("y"), lax.axis_index("z")
    copies = []
    for piece, (dys, dz, row) in zip(pieces, places):
        for index, dy in enumerate(dys):
            target = out_ref.at[
                lax.rem(y + dy, NY), lax.rem(z + dz + NZ, NZ), pl.ds(row, piece.shape[1])
            ]
            copies.append(pltpu.make_async_copy(piece.at[index], target, sems.at[len(copies)]))
            copies[-1].start()
    for copy in copies:
        copy.wait()


def place(out, width, items):
    pieces = near(*(piece for piece, _ in items))
    places = [where for _, where in items]
    n = len(pieces)
    aliased = out is not None
    return pl.pallas_call(
        functools.partial(place_kernel, places, n, int(aliased)),
        out_shape=jax.ShapeDtypeStruct((NY, NZ, COLS, width), jnp.bfloat16),
        in_specs=[VMEM] * n + [ANY] * aliased,
        out_specs=ANY,
        scratch_shapes=[pltpu.SemaphoreType.DMA((sum(len(w[0]) for w in places),))],
        input_output_aliases={n: 0} if aliased else {},
        compiler_params=pltpu.CompilerParams(vmem_limit_bytes=4 << 20),
    )(*pieces, *([out] if aliased else []))


def move(value, axis, size, by):
    return lax.ppermute(value, axis, shift(size, by))


def body(x, g, counts):
    width = g.shape[2]

    far_hbm = functools.partial(pltpu.with_memory_space_constraint, memory_space=pltpu.HBM)
    *sides, mine = pl.pallas_call(
        pack_kernel,
        out_shape=[pltpu.VMEM((NZ, COLS, CAP), jnp.bfloat16)] * NY
        + [pltpu.VMEM((NZ, BLK, width), jnp.bfloat16)],
        in_specs=[SMEM, ANY, ANY],
        out_specs=[VMEM] * (NY + 1),
        scratch_shapes=[pltpu.SemaphoreType.DMA((NY + 1,))],
        compiler_params=pltpu.CompilerParams(vmem_limit_bytes=2 << 20),
        name="pack",
    )(
        counts,
        far_hbm(x.transpose(0, 2, 1).reshape(NY, NZ, COLS, CAP)),
        far_hbm(g.reshape(NY, NZ, CAP // BLK, BLK, width)),
    )
    sides = [sides[0]] + [move(sides[k], "y", NY, SIDES[k]) for k in range(1, NY)]
    own = lax.all_to_all(mine, "z", 0, 0, tiled=True)
    xz = lax.all_to_all(jnp.stack(sides, axis=1), "z", 0, 0, tiled=True)

    right = move(own, "x", NX, 1)
    left = move(own, "x", NX, -1)
    far_a = move(right[: NZ // 2], "x", NX, 1)
    far_b = move(left[NZ // 2 :], "x", NX, -1)
    pieces = [own, right, left, far_a, far_b]
    pieces = pieces + [move(p, "c", NC, 1) for p in pieces]

    grad = pl.pallas_call(
        grad_kernel,
        out_shape=pltpu.VMEM((NY * COLS, width), jnp.bfloat16),
        in_specs=[VMEM] * 11,
        out_specs=VMEM,
        scratch_shapes=[pltpu.VMEM((NZ, CAP // BLK, BLK, width), jnp.bfloat16)],
        compiler_params=pltpu.CompilerParams(vmem_limit_bytes=12 << 20),
        name="grad",
    )(*near(xz, *pieces))

    mid = NY * COLS // 2
    right = move(grad, "x", NX, 1)
    left = move(grad, "x", NX, -1)
    total = gram_of(grad)
    far_a = move(right[:mid], "x", NX, 1)
    far_b = move(left[mid:], "x", NX, -1)
    total = total + (gram_of(right) + gram_of(left))
    other = move(total, "c", NC, 1)
    other_far_a = move(far_a, "c", NC, 1)
    other_far_b = move(far_b, "c", NC, 1)
    total = total + (gram_of(far_a) + gram_of(far_b))

    pieces = pl.pallas_call(
        functools.partial(newton_kernel, math.sqrt(2048)),
        out_shape=[pltpu.VMEM((1, COLS, width), jnp.bfloat16)] * NY,
        in_specs=[VMEM] * 5,
        out_specs=[VMEM] * NY,
        compiler_params=pltpu.CompilerParams(vmem_limit_bytes=32 << 20),
        name="newton",
    )(*near(total, other, other_far_a, other_far_b, grad))

    moved = [move(pieces[k], "y", NY, -SIDES[k]) for k in range(1, NY)]
    half = COLS // 2
    a_dys, b_dys = (0,), SIDES[1:]

    def step(right, left):
        return [move(right, "z", NZ, 1), move(left, "z", NZ, -1)]

    def halves(right, left):
        return step(right[:, :half], left[:, half:])

    a1 = step(pieces[0], pieces[0])
    a2 = step(*a1)
    *moved, a2[0], a2[1] = lax.optimization_barrier((*moved, *a2))
    moved = jnp.stack([m[0] for m in moved])
    a3 = step(*a2)
    b1 = step(moved, moved)
    *a3, b1[0], b1[1] = lax.optimization_barrier((*a3, *b1))
    a4 = halves(*a3)
    b2 = step(*b1)
    *a4, b2[0], b2[1] = lax.optimization_barrier((*a4, *b2))
    b3 = step(*b2)
    b4 = halves(*b3)

    def items(pair, dys, n):
        if n == 4:
            return [(pair[0], (dys, 4, 0)), (pair[1], (dys, 4, half))]
        return [(pair[0], (dys, -n, 0)), (pair[1], (dys, n, 0))]

    out = place(
        None,
        width,
        [(pieces[0], (a_dys, 0, 0)), (moved, (b_dys, 0, 0))]
        + items(a1, a_dys, 1)
        + items(a2, a_dys, 2)
        + items(a3, a_dys, 3)
        + items(b1, b_dys, 1),
    )
    out = place(out, width, items(a4, a_dys, 4) + items(b2, b_dys, 2) + items(b3, b_dys, 3))
    out = place(out, width, items(b4, b_dys, 4))
    return out.reshape(NY * NZ, COLS, width)


def solution(mesh):
    fine = Mesh(mesh.devices.reshape(NZ, NY, NX, NC), ("z", "y", "x", "c"))
    return jax.shard_map(
        body,
        mesh=fine,
        in_specs=(P(None, "z", ("y", "x", "c")), P(None, "z", None), P("z", None)),
        out_specs=P(None, ("y", "x", "c"), None),
        check_vma=False,
    )
```

```python
import functools
import math

import jax
import jax.numpy as jnp
from jax import lax
from jax.experimental import pallas as pl
from jax.experimental.pallas import tpu as pltpu
from jax.sharding import Mesh, PartitionSpec as P

BLK = 16
NEWTON_FIRST = 3.4445
NEWTON_SECOND = -4.775
NEWTON_THIRD = 2.0315
EPSILON = 1e-07


NZ, NY, NX, NC = 8, 4, 4, 2
COLS, CAP = 64, 128
SIDES = (0, 1, 3, 2)

VMEM = pl.BlockSpec(memory_space=pltpu.VMEM)
ANY = pl.BlockSpec(memory_space=pl.ANY)


def shift(n, k):
    return [(i, (i + k) % n) for i in range(n)]


def near(*arrays):
    return [pltpu.with_memory_space_constraint(a, pltpu.VMEM) for a in arrays]


def dot(a, b):
    return jnp.dot(a, b, preferred_element_type=jnp.float32)


def gram_of(rows):
    return lax.dot_general(rows, rows, (((0,), (0,)), ((), ())), preferred_element_type=jnp.float32)


def pack_kernel(count_hbm, x_ref, g_ref, *refs):
    x_outs, g_out, count_ref, sems = refs[:NY], *refs[NY:]
    y = lax.axis_index("y")
    block = NC * lax.axis_index("x") + lax.axis_index("c")
    copies = [
        pltpu.make_async_copy(g_ref.at[y, :, block], g_out, sems.at[NY]),
        pltpu.make_async_copy(count_hbm, count_ref, sems.at[NY + 1]),
    ]
    for k, dy in enumerate(SIDES):
        source = x_ref.at[lax.rem(y + dy, NY)]
        copies.append(pltpu.make_async_copy(source, x_outs[k], sems.at[k]))
    for copy in copies:
        copy.start()
    for copy in copies:
        copy.wait()
    for plane in range(NZ):

        @pl.when(block >= count_ref[0, NZ * y + plane])
        def _():
            g_out[plane] = jnp.zeros(g_out.shape[1:], g_out.dtype)


def grad_kernel(xt_ref, *refs):
    pieces, out_ref, rows = refs[:-2], refs[-2], refs[-1]
    x, c = lax.axis_index("x"), lax.axis_index("c")
    half = NZ // 2
    for core in range(NC):
        own, right, left, far_a, far_b = pieces[5 * core : 5 * core + 5]
        for offset, ref, first in (
            (0, own, 0),
            (3, right, 0),
            (1, left, 0),
            (2, far_a, 0),
            (2, far_b, half),
        ):
            block = NC * lax.rem(x + offset, NX) + (c if core == 0 else 1 - c)
            for r in range(ref.shape[0]):
                rows[first + r, block] = ref[r]
    total = None
    for r in range(0, NZ, 2):
        lhs = jnp.concatenate(
            [xt_ref[r].reshape(NY * COLS, CAP), xt_ref[r + 1].reshape(NY * COLS, CAP)], axis=1
        )
        part = dot(lhs, rows[r : r + 2].reshape(2 * CAP, rows.shape[-1]))
        total = part if total is None else total + part
    out_ref[...] = total.astype(jnp.bfloat16)


def newton_kernel(scale, mine_ref, other_ref, far_a_ref, far_b_ref, grad_ref, *out_refs):
    far = jnp.concatenate([far_a_ref[...], far_b_ref[...]], axis=0)
    raw = mine_ref[...] + other_ref[...] + gram_of(far)
    n = raw.shape[0]
    diagonal = lax.broadcasted_iota(jnp.int32, (n, n), 0) == lax.broadcasted_iota(
        jnp.int32, (n, n), 1
    )
    norm = jnp.sqrt(jnp.sum(jnp.where(diagonal, raw, 0.0), keepdims=True))
    inverse = 1.0 / (norm + EPSILON)
    gram = raw * inverse * inverse
    gram16 = gram.astype(jnp.bfloat16)
    first = (NEWTON_SECOND * gram + NEWTON_THIRD * dot(gram16, gram16)).astype(jnp.bfloat16)
    grad = grad_ref[...]
    current = inverse * (NEWTON_FIRST * grad.astype(jnp.float32) + dot(grad, first))
    half = NEWTON_FIRST * gram + dot(first, gram16)
    gram = NEWTON_FIRST * half + dot(half.astype(jnp.bfloat16), first)
    gram16 = gram.astype(jnp.bfloat16)
    second = (NEWTON_SECOND * gram + NEWTON_THIRD * dot(gram16, gram16)).astype(jnp.bfloat16)
    out = NEWTON_FIRST * current + dot(current.astype(jnp.bfloat16), second)
    out = (scale * out).astype(jnp.bfloat16)
    for k in range(NY):
        out_refs[k][...] = out[COLS * k : COLS * (k + 1)].reshape(out_refs[k].shape)


def place_kernel(places, n, aliased, *refs):
    pieces, (out_ref, sems) = refs[:n], refs[n + aliased :]
    y, z = lax.axis_index("y"), lax.axis_index("z")
    copies = []
    for piece, (dys, dz, row) in zip(pieces, places):
        for index, dy in enumerate(dys):
            target = out_ref.at[
                lax.rem(y + dy, NY), lax.rem(z + dz + NZ, NZ), pl.ds(row, piece.shape[1])
            ]
            copies.append(pltpu.make_async_copy(piece.at[index], target, sems.at[len(copies)]))
            copies[-1].start()
    for copy in copies:
        copy.wait()


def place(out, width, items):
    pieces = near(*(piece for piece, _ in items))
    places = [where for _, where in items]
    n = len(pieces)
    aliased = out is not None
    return pl.pallas_call(
        functools.partial(place_kernel, places, n, int(aliased)),
        out_shape=jax.ShapeDtypeStruct((NY, NZ, COLS, width), jnp.bfloat16),
        in_specs=[VMEM] * n + [ANY] * aliased,
        out_specs=ANY,
        scratch_shapes=[pltpu.SemaphoreType.DMA((sum(len(w[0]) for w in places),))],
        input_output_aliases={n: 0} if aliased else {},
        compiler_params=pltpu.CompilerParams(vmem_limit_bytes=4 << 20),
    )(*pieces, *([out] if aliased else []))


def move(value, axis, size, by):
    return lax.ppermute(value, axis, shift(size, by))


def body(x, g, counts):
    width = g.shape[2]

    far_hbm = functools.partial(pltpu.with_memory_space_constraint, memory_space=pltpu.HBM)
    *sides, mine = pl.pallas_call(
        pack_kernel,
        out_shape=[pltpu.VMEM((NZ, COLS, CAP), jnp.bfloat16)] * NY
        + [pltpu.VMEM((NZ, BLK, width), jnp.bfloat16)],
        in_specs=[ANY] * 3,
        out_specs=[VMEM] * (NY + 1),
        scratch_shapes=[
            pltpu.SMEM((1, NY * NZ), jnp.int32),
            pltpu.SemaphoreType.DMA((NY + 2,)),
        ],
        compiler_params=pltpu.CompilerParams(vmem_limit_bytes=2 << 20),
        name="pack",
    )(
        far_hbm(counts),
        far_hbm(x.transpose(0, 2, 1).reshape(NY, NZ, COLS, CAP)),
        far_hbm(g.reshape(NY, NZ, CAP // BLK, BLK, width)),
    )
    sides = [sides[0]] + [move(sides[k], "y", NY, SIDES[k]) for k in range(1, NY)]
    sides = jnp.stack(sides, axis=1)
    own = lax.all_to_all(mine, "z", 0, 0, tiled=True)
    xz = lax.all_to_all(sides, "z", 0, 0, tiled=True)

    right = move(own, "x", NX, 1)
    left = move(own, "x", NX, -1)
    far_a = move(right[: NZ // 2], "x", NX, 1)
    far_b = move(left[NZ // 2 :], "x", NX, -1)
    pieces = [own, right, left, far_a, far_b]
    pieces = pieces + [move(p, "c", NC, 1) for p in pieces]

    grad = pl.pallas_call(
        grad_kernel,
        out_shape=pltpu.VMEM((NY * COLS, width), jnp.bfloat16),
        in_specs=[VMEM] * 11,
        out_specs=VMEM,
        scratch_shapes=[pltpu.VMEM((NZ, CAP // BLK, BLK, width), jnp.bfloat16)],
        compiler_params=pltpu.CompilerParams(vmem_limit_bytes=12 << 20),
        name="grad",
    )(*near(xz, *pieces))

    mid = NY * COLS // 2
    right = move(grad, "x", NX, 1)
    left = move(grad, "x", NX, -1)
    total = gram_of(grad)
    far_a = move(right[:mid], "x", NX, 1)
    far_b = move(left[mid:], "x", NX, -1)
    total = total + (gram_of(right) + gram_of(left))
    other = move(total, "c", NC, 1)
    other_far_a = move(far_a, "c", NC, 1)
    other_far_b = move(far_b, "c", NC, 1)
    total = total + (gram_of(far_a) + gram_of(far_b))

    pieces = pl.pallas_call(
        functools.partial(newton_kernel, math.sqrt(2048)),
        out_shape=[pltpu.VMEM((1, COLS, width), jnp.bfloat16)] * NY,
        in_specs=[VMEM] * 5,
        out_specs=[VMEM] * NY,
        compiler_params=pltpu.CompilerParams(vmem_limit_bytes=32 << 20),
        name="newton",
    )(*near(total, other, other_far_a, other_far_b, grad))

    rows = [pieces[0]] + [move(pieces[k], "y", NY, -SIDES[k]) for k in range(1, NY)]
    rows = jnp.stack([r[0] for r in rows])
    right, left = rows, rows
    items = [[(rows, (SIDES, 0, 0))]]
    for n in range(1, 4):
        right = move(right, "z", NZ, 1)
        left = move(left, "z", NZ, -1)
        items.append([(right, (SIDES, -n, 0)), (left, (SIDES, n, 0))])
    half = COLS // 2
    right = move(right[:, :half], "z", NZ, 1)
    left = move(left[:, half:], "z", NZ, -1)
    out = place(None, width, items[0] + items[1] + items[2])
    out = place(out, width, items[3])
    out = place(out, width, [(right, (SIDES, 4, 0)), (left, (SIDES, 4, half))])
    return out.reshape(NY * NZ, COLS, width)


def solution(mesh):
    fine = Mesh(mesh.devices.reshape(NZ, NY, NX, NC), ("z", "y", "x", "c"))
    return jax.shard_map(
        body,
        mesh=fine,
        in_specs=(P(None, "z", ("y", "x", "c")), P(None, "z", None), P("z", None)),
        out_specs=P(None, ("y", "x", "c"), None),
        check_vma=False,
    )
```

```python
import functools
import math

import jax
import jax.numpy as jnp
from jax import lax
from jax.experimental import pallas as pl
from jax.experimental.pallas import tpu as pltpu
from jax.sharding import Mesh, PartitionSpec as P

BLK = 16
NEWTON_FIRST = 3.4445
NEWTON_SECOND = -4.775
NEWTON_THIRD = 2.0315
EPSILON = 1e-07


NZ, NY, NX, NC = 8, 4, 4, 2
COLS, CAP = 64, 128
SIDES = (0, 1, 3, 2)
CHUNKS = ((0, 1), (2, 3))

VMEM = pl.BlockSpec(memory_space=pltpu.VMEM)
ANY = pl.BlockSpec(memory_space=pl.ANY)


def shift(n, k):
    return [(i, (i + k) % n) for i in range(n)]


def near(*arrays):
    return [pltpu.with_memory_space_constraint(a, pltpu.VMEM) for a in arrays]


def dot(a, b):
    return jnp.dot(a, b, preferred_element_type=jnp.float32)


def gram_of(rows):
    return lax.dot_general(rows, rows, (((0,), (0,)), ((), ())), preferred_element_type=jnp.float32)


def pack_kernel(count_hbm, x_ref, g_ref, *refs):
    x_outs, g_out, count_ref, sems = refs[:NY], *refs[NY:]
    y = lax.axis_index("y")
    block = NC * lax.axis_index("x") + lax.axis_index("c")
    copies = [
        pltpu.make_async_copy(g_ref.at[y, :, block], g_out, sems.at[NY]),
        pltpu.make_async_copy(count_hbm, count_ref, sems.at[NY + 1]),
    ]
    for k, dy in enumerate(SIDES):
        source = x_ref.at[lax.rem(y + dy, NY)]
        copies.append(pltpu.make_async_copy(source, x_outs[k], sems.at[k]))
    for copy in copies:
        copy.start()
    for copy in copies:
        copy.wait()
    for plane in range(NZ):

        @pl.when(block >= count_ref[0, NZ * y + plane])
        def _():
            g_out[plane] = jnp.zeros(g_out.shape[1:], g_out.dtype)


def grad_kernel(xt_ref, *refs):
    pieces, out_ref, rows = refs[:-2], refs[-2], refs[-1]
    x, c = lax.axis_index("x"), lax.axis_index("c")
    half = NZ // 2
    for core in range(NC):
        own, right, left, far_a, far_b = pieces[5 * core : 5 * core + 5]
        for offset, ref, first in (
            (0, own, 0),
            (3, right, 0),
            (1, left, 0),
            (2, far_a, 0),
            (2, far_b, half),
        ):
            block = NC * lax.rem(x + offset, NX) + (c if core == 0 else 1 - c)
            for r in range(ref.shape[0]):
                rows[first + r, block] = ref[r]
    total = None
    for r in range(0, NZ, 2):
        lhs = jnp.concatenate(
            [xt_ref[r].reshape(NY * COLS, CAP), xt_ref[r + 1].reshape(NY * COLS, CAP)], axis=1
        )
        part = dot(lhs, rows[r : r + 2].reshape(2 * CAP, rows.shape[-1]))
        total = part if total is None else total + part
    out_ref[...] = total.astype(jnp.bfloat16)


def newton_kernel(scale, mine_ref, other_ref, far_a_ref, far_b_ref, grad_ref, *out_refs):
    far = jnp.concatenate([far_a_ref[...], far_b_ref[...]], axis=0)
    raw = mine_ref[...] + other_ref[...] + gram_of(far)
    n = raw.shape[0]
    diagonal = lax.broadcasted_iota(jnp.int32, (n, n), 0) == lax.broadcasted_iota(
        jnp.int32, (n, n), 1
    )
    norm = jnp.sqrt(jnp.sum(jnp.where(diagonal, raw, 0.0), keepdims=True))
    inverse = 1.0 / (norm + EPSILON)
    gram = raw * inverse * inverse
    gram16 = gram.astype(jnp.bfloat16)
    first = (NEWTON_SECOND * gram + NEWTON_THIRD * dot(gram16, gram16)).astype(jnp.bfloat16)
    grad = grad_ref[...]
    current = inverse * (NEWTON_FIRST * grad.astype(jnp.float32) + dot(grad, first))
    half = NEWTON_FIRST * gram + dot(first, gram16)
    gram = NEWTON_FIRST * half + dot(half.astype(jnp.bfloat16), first)
    gram16 = gram.astype(jnp.bfloat16)
    second = (NEWTON_SECOND * gram + NEWTON_THIRD * dot(gram16, gram16)).astype(jnp.bfloat16)
    out = NEWTON_FIRST * current + dot(current.astype(jnp.bfloat16), second)
    out = (scale * out).astype(jnp.bfloat16)
    for k in range(NY):
        out_refs[k][...] = out[COLS * k : COLS * (k + 1)].reshape(out_refs[k].shape)


def place_kernel(places, n, aliased, *refs):
    pieces, (out_ref, sems) = refs[:n], refs[n + aliased :]
    y, z = lax.axis_index("y"), lax.axis_index("z")
    copies = []
    for piece, (dys, dz, row) in zip(pieces, places):
        for index, dy in enumerate(dys):
            target = out_ref.at[
                lax.rem(y + dy, NY), lax.rem(z + dz + NZ, NZ), pl.ds(row, piece.shape[1])
            ]
            copies.append(pltpu.make_async_copy(piece.at[index], target, sems.at[len(copies)]))
            copies[-1].start()
    for copy in copies:
        copy.wait()


def place(out, width, items):
    pieces = near(*(piece for piece, _ in items))
    places = [where for _, where in items]
    n = len(pieces)
    aliased = out is not None
    return pl.pallas_call(
        functools.partial(place_kernel, places, n, int(aliased)),
        out_shape=jax.ShapeDtypeStruct((NY, NZ, COLS, width), jnp.bfloat16),
        in_specs=[VMEM] * n + [ANY] * aliased,
        out_specs=ANY,
        scratch_shapes=[pltpu.SemaphoreType.DMA((sum(len(w[0]) for w in places),))],
        input_output_aliases={n: 0} if aliased else {},
        compiler_params=pltpu.CompilerParams(vmem_limit_bytes=4 << 20),
    )(*pieces, *([out] if aliased else []))


def move(value, axis, size, by):
    return lax.ppermute(value, axis, shift(size, by))


def body(x, g, counts):
    width = g.shape[2]

    far_hbm = functools.partial(pltpu.with_memory_space_constraint, memory_space=pltpu.HBM)
    *sides, mine = pl.pallas_call(
        pack_kernel,
        out_shape=[pltpu.VMEM((NZ, COLS, CAP), jnp.bfloat16)] * NY
        + [pltpu.VMEM((NZ, BLK, width), jnp.bfloat16)],
        in_specs=[ANY] * 3,
        out_specs=[VMEM] * (NY + 1),
        scratch_shapes=[
            pltpu.SMEM((1, NY * NZ), jnp.int32),
            pltpu.SemaphoreType.DMA((NY + 2,)),
        ],
        compiler_params=pltpu.CompilerParams(vmem_limit_bytes=2 << 20),
        name="pack",
    )(
        far_hbm(counts),
        far_hbm(x.transpose(0, 2, 1).reshape(NY, NZ, COLS, CAP)),
        far_hbm(g.reshape(NY, NZ, CAP // BLK, BLK, width)),
    )
    sides = [sides[0]] + [move(sides[k], "y", NY, SIDES[k]) for k in range(1, NY)]
    sides = jnp.stack(sides, axis=1)
    own = lax.all_to_all(mine, "z", 0, 0, tiled=True)
    xz = lax.all_to_all(sides, "z", 0, 0, tiled=True)

    right = move(own, "x", NX, 1)
    left = move(own, "x", NX, -1)
    far_a = move(right[: NZ // 2], "x", NX, 1)
    far_b = move(left[NZ // 2 :], "x", NX, -1)
    pieces = [own, right, left, far_a, far_b]
    pieces = pieces + [move(p, "c", NC, 1) for p in pieces]

    grad = pl.pallas_call(
        grad_kernel,
        out_shape=pltpu.VMEM((NY * COLS, width), jnp.bfloat16),
        in_specs=[VMEM] * 11,
        out_specs=VMEM,
        scratch_shapes=[pltpu.VMEM((NZ, CAP // BLK, BLK, width), jnp.bfloat16)],
        compiler_params=pltpu.CompilerParams(vmem_limit_bytes=12 << 20),
        name="grad",
    )(*near(xz, *pieces))

    mid = NY * COLS // 2
    right = move(grad, "x", NX, 1)
    left = move(grad, "x", NX, -1)
    total = gram_of(grad)
    far_a = move(right[:mid], "x", NX, 1)
    far_b = move(left[mid:], "x", NX, -1)
    total = total + (gram_of(right) + gram_of(left))
    other = move(total, "c", NC, 1)
    other_far_a = move(far_a, "c", NC, 1)
    other_far_b = move(far_b, "c", NC, 1)
    total = total + (gram_of(far_a) + gram_of(far_b))

    pieces = pl.pallas_call(
        functools.partial(newton_kernel, math.sqrt(2048)),
        out_shape=[pltpu.VMEM((1, COLS, width), jnp.bfloat16)] * NY,
        in_specs=[VMEM] * 5,
        out_specs=[VMEM] * NY,
        compiler_params=pltpu.CompilerParams(vmem_limit_bytes=32 << 20),
        name="newton",
    )(*near(total, other, other_far_a, other_far_b, grad))

    rows = [pieces[0]] + [move(pieces[k], "y", NY, -SIDES[k]) for k in range(1, NY)]
    half = COLS // 2
    items = []
    for ks in CHUNKS:
        piece = jnp.stack([rows[k][0] for k in ks])
        dys = tuple(SIDES[k] for k in ks)
        items.append([(piece, (dys, 0, 0))])
        right, left = piece, piece
        for n in range(1, 4):
            right = move(right, "z", NZ, 1)
            left = move(left, "z", NZ, -1)
            items[-1] += [(right, (dys, -n, 0)), (left, (dys, n, 0))]
        right = move(right[:, :half], "z", NZ, 1)
        left = move(left[:, half:], "z", NZ, -1)
        items[-1] += [(right, (dys, 4, 0)), (left, (dys, 4, half))]
    a, b = items
    out = place(None, width, a[:5] + b[:3])
    out = place(out, width, a[5:7] + b[3:5])
    out = place(out, width, a[7:] + b[5:7])
    out = place(out, width, b[7:])
    return out.reshape(NY * NZ, COLS, width)


def solution(mesh):
    fine = Mesh(mesh.devices.reshape(NZ, NY, NX, NC), ("z", "y", "x", "c"))
    return jax.shard_map(
        body,
        mesh=fine,
        in_specs=(P(None, "z", ("y", "x", "c")), P(None, "z", None), P("z", None)),
        out_specs=P(None, ("y", "x", "c"), None),
        check_vma=False,
    )
```

```python
import functools
import math

import jax
import jax.numpy as jnp
from jax import lax
from jax.experimental import pallas as pl
from jax.experimental.pallas import tpu as pltpu
from jax.sharding import Mesh, PartitionSpec as P

BLK = 16
NEWTON_FIRST = 3.4445
NEWTON_SECOND = -4.775
NEWTON_THIRD = 2.0315
EPSILON = 1e-07


NZ, NY, NX, NC = 8, 4, 4, 2
COLS, CAP = 64, 128
SIDES = (0, 1, 3, 2)
CHUNKS = ((0, 1), (2, 3))

VMEM = pl.BlockSpec(memory_space=pltpu.VMEM)
ANY = pl.BlockSpec(memory_space=pl.ANY)


def shift(n, k):
    return [(i, (i + k) % n) for i in range(n)]


def pair(n, mask):
    return [(i, i ^ mask) for i in range(n)]


def near(*arrays):
    return [pltpu.with_memory_space_constraint(a, pltpu.VMEM) for a in arrays]


def dot(a, b):
    return jnp.dot(a, b, preferred_element_type=jnp.float32)


def gram_of(rows):
    return lax.dot_general(rows, rows, (((0,), (0,)), ((), ())), preferred_element_type=jnp.float32)


def pack_kernel(count_hbm, x_ref, g_ref, *refs):
    x_outs, g_out, count_ref, sems = refs[:NY], *refs[NY:]
    y = lax.axis_index("y")
    block = NC * lax.axis_index("x") + lax.axis_index("c")
    copies = [
        pltpu.make_async_copy(g_ref.at[y, :, block], g_out, sems.at[NY]),
        pltpu.make_async_copy(count_hbm, count_ref, sems.at[NY + 1]),
    ]
    for k, mask in enumerate(SIDES):
        source = x_ref.at[y ^ mask]
        copies.append(pltpu.make_async_copy(source, x_outs[k], sems.at[k]))
    for copy in copies:
        copy.start()
    for copy in copies:
        copy.wait()
    for plane in range(NZ):

        @pl.when(block >= count_ref[0, NZ * y + plane])
        def _():
            g_out[plane] = jnp.zeros(g_out.shape[1:], g_out.dtype)


def grad_kernel(xt_ref, *refs):
    pieces, out_ref, rows = refs[:-2], refs[-2], refs[-1]
    x, c = lax.axis_index("x"), lax.axis_index("c")
    half = NZ // 2
    for core in range(NC):
        own, near_1, near_3, far_a, far_b = pieces[5 * core : 5 * core + 5]
        for mask, ref, first in (
            (0, own, 0),
            (1, near_1, 0),
            (3, near_3, 0),
            (2, far_a, 0),
            (2, far_b, half),
        ):
            block = NC * (x ^ mask) + (c if core == 0 else 1 - c)
            for r in range(ref.shape[0]):
                rows[first + r, block] = ref[r]
    total = None
    for r in range(0, NZ, 2):
        lhs = jnp.concatenate(
            [xt_ref[r].reshape(NY * COLS, CAP), xt_ref[r + 1].reshape(NY * COLS, CAP)], axis=1
        )
        part = dot(lhs, rows[r : r + 2].reshape(2 * CAP, rows.shape[-1]))
        total = part if total is None else total + part
    out_ref[...] = total.astype(jnp.bfloat16)


def newton_kernel(scale, mine_ref, other_ref, far_a_ref, far_b_ref, grad_ref, *out_refs):
    far = jnp.concatenate([far_a_ref[...], far_b_ref[...]], axis=0)
    raw = mine_ref[...] + other_ref[...] + gram_of(far)
    n = raw.shape[0]
    diagonal = lax.broadcasted_iota(jnp.int32, (n, n), 0) == lax.broadcasted_iota(
        jnp.int32, (n, n), 1
    )
    norm = jnp.sqrt(jnp.sum(jnp.where(diagonal, raw, 0.0), keepdims=True))
    inverse = 1.0 / (norm + EPSILON)
    gram = raw * inverse * inverse
    gram16 = gram.astype(jnp.bfloat16)
    first = (NEWTON_SECOND * gram + NEWTON_THIRD * dot(gram16, gram16)).astype(jnp.bfloat16)
    grad = grad_ref[...]
    current = inverse * (NEWTON_FIRST * grad.astype(jnp.float32) + dot(grad, first))
    half = NEWTON_FIRST * gram + dot(first, gram16)
    gram = NEWTON_FIRST * half + dot(half.astype(jnp.bfloat16), first)
    gram16 = gram.astype(jnp.bfloat16)
    second = (NEWTON_SECOND * gram + NEWTON_THIRD * dot(gram16, gram16)).astype(jnp.bfloat16)
    out = NEWTON_FIRST * current + dot(current.astype(jnp.bfloat16), second)
    out = (scale * out).astype(jnp.bfloat16)
    for k in range(NY):
        out_refs[k][...] = out[COLS * k : COLS * (k + 1)].reshape(out_refs[k].shape)


def place_kernel(places, n, aliased, *refs):
    pieces, (out_ref, sems) = refs[:n], refs[n + aliased :]
    y, z = lax.axis_index("y"), lax.axis_index("z")
    copies = []
    for piece, (masks, dz, row) in zip(pieces, places):
        for index, mask in enumerate(masks):
            target = out_ref.at[
                y ^ mask, lax.rem(z + dz + NZ, NZ), pl.ds(row, piece.shape[1])
            ]
            copies.append(pltpu.make_async_copy(piece.at[index], target, sems.at[len(copies)]))
            copies[-1].start()
    for copy in copies:
        copy.wait()


def place(out, width, items):
    pieces = near(*(piece for piece, _ in items))
    places = [where for _, where in items]
    n = len(pieces)
    aliased = out is not None
    return pl.pallas_call(
        functools.partial(place_kernel, places, n, int(aliased)),
        out_shape=jax.ShapeDtypeStruct((NY, NZ, COLS, width), jnp.bfloat16),
        in_specs=[VMEM] * n + [ANY] * aliased,
        out_specs=ANY,
        scratch_shapes=[pltpu.SemaphoreType.DMA((sum(len(w[0]) for w in places),))],
        input_output_aliases={n: 0} if aliased else {},
        compiler_params=pltpu.CompilerParams(vmem_limit_bytes=4 << 20),
    )(*pieces, *([out] if aliased else []))


def move(value, axis, to):
    return lax.ppermute(value, axis, to)


def body(x, g, counts):
    width = g.shape[2]

    far_hbm = functools.partial(pltpu.with_memory_space_constraint, memory_space=pltpu.HBM)
    *sides, mine = pl.pallas_call(
        pack_kernel,
        out_shape=[pltpu.VMEM((NZ, COLS, CAP), jnp.bfloat16)] * NY
        + [pltpu.VMEM((NZ, BLK, width), jnp.bfloat16)],
        in_specs=[ANY] * 3,
        out_specs=[VMEM] * (NY + 1),
        scratch_shapes=[
            pltpu.SMEM((1, NY * NZ), jnp.int32),
            pltpu.SemaphoreType.DMA((NY + 2,)),
        ],
        compiler_params=pltpu.CompilerParams(vmem_limit_bytes=2 << 20),
        name="pack",
    )(
        far_hbm(counts),
        far_hbm(x.transpose(0, 2, 1).reshape(NY, NZ, COLS, CAP)),
        far_hbm(g.reshape(NY, NZ, CAP // BLK, BLK, width)),
    )
    sides = [sides[0]] + [move(sides[k], "y", pair(NY, SIDES[k])) for k in range(1, NY)]
    sides = jnp.stack(sides, axis=1)
    own = lax.all_to_all(mine, "z", 0, 0, tiled=True)
    xz = lax.all_to_all(sides, "z", 0, 0, tiled=True)

    near_1 = move(own, "x", pair(NX, 1))
    near_3 = move(own, "x", pair(NX, 3))
    far_a = move(near_3[: NZ // 2], "x", pair(NX, 1))
    far_b = move(near_1[NZ // 2 :], "x", pair(NX, 3))
    pieces = [own, near_1, near_3, far_a, far_b]
    pieces = pieces + [move(p, "c", pair(NC, 1)) for p in pieces]

    grad = pl.pallas_call(
        grad_kernel,
        out_shape=pltpu.VMEM((NY * COLS, width), jnp.bfloat16),
        in_specs=[VMEM] * 11,
        out_specs=VMEM,
        scratch_shapes=[pltpu.VMEM((NZ, CAP // BLK, BLK, width), jnp.bfloat16)],
        compiler_params=pltpu.CompilerParams(vmem_limit_bytes=12 << 20),
        name="grad",
    )(*near(xz, *pieces))

    mid = NY * COLS // 2
    near_1 = move(grad, "x", pair(NX, 1))
    near_3 = move(grad, "x", pair(NX, 3))
    total = gram_of(grad)
    far_a = move(near_3[:mid], "x", pair(NX, 1))
    far_b = move(near_1[mid:], "x", pair(NX, 3))
    total = total + (gram_of(near_1) + gram_of(near_3))
    other = move(total, "c", pair(NC, 1))
    other_far_a = move(far_a, "c", pair(NC, 1))
    other_far_b = move(far_b, "c", pair(NC, 1))
    total = total + (gram_of(far_a) + gram_of(far_b))

    pieces = pl.pallas_call(
        functools.partial(newton_kernel, math.sqrt(2048)),
        out_shape=[pltpu.VMEM((1, COLS, width), jnp.bfloat16)] * NY,
        in_specs=[VMEM] * 5,
        out_specs=[VMEM] * NY,
        compiler_params=pltpu.CompilerParams(vmem_limit_bytes=32 << 20),
        name="newton",
    )(*near(total, other, other_far_a, other_far_b, grad))

    rows = [pieces[0]] + [move(pieces[k], "y", pair(NY, SIDES[k])) for k in range(1, NY)]
    half = COLS // 2
    items = []
    for ks in CHUNKS:
        piece = jnp.stack([rows[k][0] for k in ks])
        masks = tuple(SIDES[k] for k in ks)
        items.append([(piece, (masks, 0, 0))])
        right, left = piece, piece
        for n in range(1, 4):
            right = move(right, "z", shift(NZ, 1))
            left = move(left, "z", shift(NZ, -1))
            items[-1] += [(right, (masks, -n, 0)), (left, (masks, n, 0))]
        right = move(right[:, :half], "z", shift(NZ, 1))
        left = move(left[:, half:], "z", shift(NZ, -1))
        items[-1] += [(right, (masks, 4, 0)), (left, (masks, 4, half))]
    a, b = items
    out = place(None, width, a[:5] + b[:3])
    out = place(out, width, a[5:7] + b[3:5])
    out = place(out, width, a[7:] + b[5:7])
    out = place(out, width, b[7:])
    return out.reshape(NY * NZ, COLS, width)


def solution(mesh):
    fine = Mesh(mesh.devices.reshape(NZ, NY, NX, NC), ("z", "y", "x", "c"))
    return jax.shard_map(
        body,
        mesh=fine,
        in_specs=(P(None, "z", ("y", "x", "c")), P(None, "z", None), P("z", None)),
        out_specs=P(None, ("y", "x", "c"), None),
        check_vma=False,
    )
```

```python
import functools
import math

import jax
import jax.numpy as jnp
from jax import lax
from jax.experimental import pallas as pl
from jax.experimental.pallas import tpu as pltpu
from jax.sharding import Mesh, PartitionSpec as P

BLK = 16
NEWTON_FIRST = 3.4445
NEWTON_SECOND = -4.775
NEWTON_THIRD = 2.0315
EPSILON = 1e-07


NZ, NY, NX, NC = 8, 4, 4, 2
COLS, CAP = 64, 128
SIDES = (0, 1, 3, 2)
CHUNKS = ((0, 1), (2, 3))

VMEM = pl.BlockSpec(memory_space=pltpu.VMEM)
ANY = pl.BlockSpec(memory_space=pl.ANY)


def pair(n, mask):
    return [(i, i ^ mask) for i in range(n)]


def link(n, odd):
    return [(i, (i + (1 if i % 2 == odd else n - 1)) % n) for i in range(n)]


def near(*arrays):
    return [pltpu.with_memory_space_constraint(a, pltpu.VMEM) for a in arrays]


def dot(a, b):
    return jnp.dot(a, b, preferred_element_type=jnp.float32)


def gram_of(rows):
    return lax.dot_general(rows, rows, (((0,), (0,)), ((), ())), preferred_element_type=jnp.float32)


def pack_kernel(count_hbm, x_ref, g_ref, *refs):
    x_outs, g_out, count_ref, sems = refs[:NY], *refs[NY:]
    y = lax.axis_index("y")
    block = NC * lax.axis_index("x") + lax.axis_index("c")
    copies = [
        pltpu.make_async_copy(g_ref.at[y, :, block], g_out, sems.at[NY]),
        pltpu.make_async_copy(count_hbm, count_ref, sems.at[NY + 1]),
    ]
    for k, mask in enumerate(SIDES):
        source = x_ref.at[y ^ mask]
        copies.append(pltpu.make_async_copy(source, x_outs[k], sems.at[k]))
    for copy in copies:
        copy.start()
    for copy in copies:
        copy.wait()
    for plane in range(NZ):

        @pl.when(block >= count_ref[0, NZ * y + plane])
        def _():
            g_out[plane] = jnp.zeros(g_out.shape[1:], g_out.dtype)


def grad_kernel(xt_ref, *refs):
    pieces, out_ref, rows = refs[:-2], refs[-2], refs[-1]
    x, c = lax.axis_index("x"), lax.axis_index("c")
    half = NZ // 2
    for core in range(NC):
        own, near_1, near_3, far_a, far_b = pieces[5 * core : 5 * core + 5]
        for mask, ref, first in (
            (0, own, 0),
            (1, near_1, 0),
            (3, near_3, 0),
            (2, far_a, 0),
            (2, far_b, half),
        ):
            block = NC * (x ^ mask) + (c if core == 0 else 1 - c)
            for r in range(ref.shape[0]):
                rows[first + r, block] = ref[r]
    total = None
    for r in range(0, NZ, 2):
        lhs = jnp.concatenate(
            [xt_ref[r].reshape(NY * COLS, CAP), xt_ref[r + 1].reshape(NY * COLS, CAP)], axis=1
        )
        part = dot(lhs, rows[r : r + 2].reshape(2 * CAP, rows.shape[-1]))
        total = part if total is None else total + part
    out_ref[...] = total.astype(jnp.bfloat16)


def newton_kernel(scale, mine_ref, other_ref, far_a_ref, far_b_ref, grad_ref, *out_refs):
    far = jnp.concatenate([far_a_ref[...], far_b_ref[...]], axis=0)
    raw = mine_ref[...] + other_ref[...] + gram_of(far)
    n = raw.shape[0]
    diagonal = lax.broadcasted_iota(jnp.int32, (n, n), 0) == lax.broadcasted_iota(
        jnp.int32, (n, n), 1
    )
    norm = jnp.sqrt(jnp.sum(jnp.where(diagonal, raw, 0.0), keepdims=True))
    inverse = 1.0 / (norm + EPSILON)
    gram = raw * inverse * inverse
    gram16 = gram.astype(jnp.bfloat16)
    first = (NEWTON_SECOND * gram + NEWTON_THIRD * dot(gram16, gram16)).astype(jnp.bfloat16)
    grad = grad_ref[...]
    current = inverse * (NEWTON_FIRST * grad.astype(jnp.float32) + dot(grad, first))
    half = NEWTON_FIRST * gram + dot(first, gram16)
    gram = NEWTON_FIRST * half + dot(half.astype(jnp.bfloat16), first)
    gram16 = gram.astype(jnp.bfloat16)
    second = (NEWTON_SECOND * gram + NEWTON_THIRD * dot(gram16, gram16)).astype(jnp.bfloat16)
    out = NEWTON_FIRST * current + dot(current.astype(jnp.bfloat16), second)
    out = (scale * out).astype(jnp.bfloat16)
    for k in range(NY):
        out_refs[k][...] = out[COLS * k : COLS * (k + 1)].reshape(out_refs[k].shape)


def place_kernel(places, n, aliased, *refs):
    pieces, (out_ref, sems) = refs[:n], refs[n + aliased :]
    y, z = lax.axis_index("y"), lax.axis_index("z")
    side = 1 - 2 * (z & 1)
    copies = []
    for piece, (masks, dz, row) in zip(pieces, places):
        for index, mask in enumerate(masks):
            target = out_ref.at[
                y ^ mask, lax.rem(z + side * dz + NZ, NZ), pl.ds(row, piece.shape[1])
            ]
            copies.append(pltpu.make_async_copy(piece.at[index], target, sems.at[len(copies)]))
            copies[-1].start()
    for copy in copies:
        copy.wait()


def place(out, width, items):
    pieces = near(*(piece for piece, _ in items))
    places = [where for _, where in items]
    n = len(pieces)
    aliased = out is not None
    return pl.pallas_call(
        functools.partial(place_kernel, places, n, int(aliased)),
        out_shape=jax.ShapeDtypeStruct((NY, NZ, COLS, width), jnp.bfloat16),
        in_specs=[VMEM] * n + [ANY] * aliased,
        out_specs=ANY,
        scratch_shapes=[pltpu.SemaphoreType.DMA((sum(len(w[0]) for w in places),))],
        input_output_aliases={n: 0} if aliased else {},
        compiler_params=pltpu.CompilerParams(vmem_limit_bytes=4 << 20),
    )(*pieces, *([out] if aliased else []))


def move(value, axis, to):
    return lax.ppermute(value, axis, to)


def body(x, g, counts):
    width = g.shape[2]

    far_hbm = functools.partial(pltpu.with_memory_space_constraint, memory_space=pltpu.HBM)
    *sides, mine = pl.pallas_call(
        pack_kernel,
        out_shape=[pltpu.VMEM((NZ, COLS, CAP), jnp.bfloat16)] * NY
        + [pltpu.VMEM((NZ, BLK, width), jnp.bfloat16)],
        in_specs=[ANY] * 3,
        out_specs=[VMEM] * (NY + 1),
        scratch_shapes=[
            pltpu.SMEM((1, NY * NZ), jnp.int32),
            pltpu.SemaphoreType.DMA((NY + 2,)),
        ],
        compiler_params=pltpu.CompilerParams(vmem_limit_bytes=2 << 20),
        name="pack",
    )(
        far_hbm(counts),
        far_hbm(x.transpose(0, 2, 1).reshape(NY, NZ, COLS, CAP)),
        far_hbm(g.reshape(NY, NZ, CAP // BLK, BLK, width)),
    )
    sides = [sides[0]] + [move(sides[k], "y", pair(NY, SIDES[k])) for k in range(1, NY)]
    sides = jnp.stack(sides, axis=1)
    own = lax.all_to_all(mine, "z", 0, 0, tiled=True)
    xz = lax.all_to_all(sides, "z", 0, 0, tiled=True)

    near_1 = move(own, "x", pair(NX, 1))
    near_3 = move(own, "x", pair(NX, 3))
    far_a = move(near_3[: NZ // 2], "x", pair(NX, 1))
    far_b = move(near_1[NZ // 2 :], "x", pair(NX, 3))
    pieces = [own, near_1, near_3, far_a, far_b]
    pieces = pieces + [move(p, "c", pair(NC, 1)) for p in pieces]

    grad = pl.pallas_call(
        grad_kernel,
        out_shape=pltpu.VMEM((NY * COLS, width), jnp.bfloat16),
        in_specs=[VMEM] * 11,
        out_specs=VMEM,
        scratch_shapes=[pltpu.VMEM((NZ, CAP // BLK, BLK, width), jnp.bfloat16)],
        compiler_params=pltpu.CompilerParams(vmem_limit_bytes=12 << 20),
        name="grad",
    )(*near(xz, *pieces))

    mid = NY * COLS // 2
    near_1 = move(grad, "x", pair(NX, 1))
    near_3 = move(grad, "x", pair(NX, 3))
    total = gram_of(grad)
    far_a = move(near_3[:mid], "x", pair(NX, 1))
    far_b = move(near_1[mid:], "x", pair(NX, 3))
    total = total + (gram_of(near_1) + gram_of(near_3))
    other = move(total, "c", pair(NC, 1))
    other_far_a = move(far_a, "c", pair(NC, 1))
    other_far_b = move(far_b, "c", pair(NC, 1))
    total = total + (gram_of(far_a) + gram_of(far_b))

    pieces = pl.pallas_call(
        functools.partial(newton_kernel, math.sqrt(2048)),
        out_shape=[pltpu.VMEM((1, COLS, width), jnp.bfloat16)] * NY,
        in_specs=[VMEM] * 5,
        out_specs=[VMEM] * NY,
        compiler_params=pltpu.CompilerParams(vmem_limit_bytes=32 << 20),
        name="newton",
    )(*near(total, other, other_far_a, other_far_b, grad))

    rows = [pieces[0]] + [move(pieces[k], "y", pair(NY, SIDES[k])) for k in range(1, NY)]
    half = COLS // 2
    items = []
    for ks in CHUNKS:
        piece = jnp.stack([rows[k][0] for k in ks])
        masks = tuple(SIDES[k] for k in ks)
        items.append([(piece, (masks, 0, 0))])
        even, odd = piece, piece
        for n in range(1, 4):
            even, odd = (move(odd, "z", link(NZ, 0)), move(even, "z", link(NZ, 1)))
            items[-1] += [(even, (masks, n, 0)), (odd, (masks, -n, 0))]
        even, odd = (move(odd[:, :half], "z", link(NZ, 0)), move(even[:, half:], "z", link(NZ, 1)))
        items[-1] += [(even, (masks, 4, 0)), (odd, (masks, -4, half))]
    a, b = items
    out = place(None, width, a[:5] + b[:3])
    out = place(out, width, a[5:7] + b[3:5])
    out = place(out, width, a[7:] + b[5:7])
    out = place(out, width, b[7:])
    return out.reshape(NY * NZ, COLS, width)


def solution(mesh):
    fine = Mesh(mesh.devices.reshape(NZ, NY, NX, NC), ("z", "y", "x", "c"))
    return jax.shard_map(
        body,
        mesh=fine,
        in_specs=(P(None, "z", ("y", "x", "c")), P(None, "z", None), P("z", None)),
        out_specs=P(None, ("y", "x", "c"), None),
        check_vma=False,
    )
```

```python
import functools
import math

import jax
import jax.numpy as jnp
from jax import lax
from jax.experimental import pallas as pl
from jax.experimental.pallas import tpu as pltpu
from jax.sharding import Mesh, PartitionSpec as P

BLK = 16
NEWTON_FIRST = 3.4445
NEWTON_SECOND = -4.775
NEWTON_THIRD = 2.0315
EPSILON = 1e-07


NZ, NY, NX, NC = 8, 4, 4, 2
COLS, CAP = 64, 128
SIDES = (0, 1, 3, 2)
CHUNKS = ((0, 1), (2, 3))

VMEM = pl.BlockSpec(memory_space=pltpu.VMEM)
ANY = pl.BlockSpec(memory_space=pl.ANY)


def pair(n, mask):
    return [(i, i ^ mask) for i in range(n)]


def link(n, odd):
    return [(i, (i + (1 if i % 2 == odd else n - 1)) % n) for i in range(n)]


def near(*arrays):
    return [pltpu.with_memory_space_constraint(a, pltpu.VMEM) for a in arrays]


def dot(a, b):
    return jnp.dot(a, b, preferred_element_type=jnp.float32)


def gram_of(rows):
    return lax.dot_general(rows, rows, (((0,), (0,)), ((), ())), preferred_element_type=jnp.float32)


def pack_kernel(count_hbm, x_ref, g_ref, *refs):
    x_outs, g_out, count_ref, sems = refs[:NY], *refs[NY:]
    y = lax.axis_index("y")
    block = NC * lax.axis_index("x") + lax.axis_index("c")
    copies = [
        pltpu.make_async_copy(g_ref.at[y, :, block], g_out, sems.at[NY]),
        pltpu.make_async_copy(count_hbm, count_ref, sems.at[NY + 1]),
    ]
    for k, mask in enumerate(SIDES):
        source = x_ref.at[y ^ mask]
        copies.append(pltpu.make_async_copy(source, x_outs[k], sems.at[k]))
    for copy in copies:
        copy.start()
    for copy in copies:
        copy.wait()
    for plane in range(NZ):

        @pl.when(block >= count_ref[0, NZ * y + plane])
        def _():
            g_out[plane] = jnp.zeros(g_out.shape[1:], g_out.dtype)


def join_kernel(*refs):
    for k in range(NY):
        refs[NY][:, k] = refs[k][...]


def grad_kernel(xt_ref, *refs):
    pieces, out_ref, rows = refs[:-2], refs[-2], refs[-1]
    x, c = lax.axis_index("x"), lax.axis_index("c")
    half = NZ // 2
    for core in range(NC):
        own, near_1, near_3, far_a, far_b = pieces[5 * core : 5 * core + 5]
        for mask, ref, first in (
            (0, own, 0),
            (1, near_1, 0),
            (3, near_3, 0),
            (2, far_a, 0),
            (2, far_b, half),
        ):
            block = NC * (x ^ mask) + (c if core == 0 else 1 - c)
            for r in range(ref.shape[0]):
                rows[first + r, block] = ref[r]
    total = None
    for r in range(0, NZ, 2):
        lhs = jnp.concatenate(
            [xt_ref[r].reshape(NY * COLS, CAP), xt_ref[r + 1].reshape(NY * COLS, CAP)], axis=1
        )
        part = dot(lhs, rows[r : r + 2].reshape(2 * CAP, rows.shape[-1]))
        total = part if total is None else total + part
    out_ref[...] = total.astype(jnp.bfloat16)


def newton_kernel(scale, mine_ref, other_ref, far_a_ref, far_b_ref, grad_ref, *out_refs):
    far = jnp.concatenate([far_a_ref[...], far_b_ref[...]], axis=0)
    raw = mine_ref[...] + other_ref[...] + gram_of(far)
    n = raw.shape[0]
    diagonal = lax.broadcasted_iota(jnp.int32, (n, n), 0) == lax.broadcasted_iota(
        jnp.int32, (n, n), 1
    )
    norm = jnp.sqrt(jnp.sum(jnp.where(diagonal, raw, 0.0), keepdims=True))
    inverse = 1.0 / (norm + EPSILON)
    gram = raw * inverse * inverse
    gram16 = gram.astype(jnp.bfloat16)
    first = (NEWTON_SECOND * gram + NEWTON_THIRD * dot(gram16, gram16)).astype(jnp.bfloat16)
    grad = grad_ref[...]
    current = inverse * (NEWTON_FIRST * grad.astype(jnp.float32) + dot(grad, first))
    half = NEWTON_FIRST * gram + dot(first, gram16)
    gram = NEWTON_FIRST * half + dot(half.astype(jnp.bfloat16), first)
    gram16 = gram.astype(jnp.bfloat16)
    once = dot(current.astype(jnp.bfloat16), gram16)
    twice = dot(once.astype(jnp.bfloat16), gram16)
    out = NEWTON_FIRST * current + NEWTON_SECOND * once + NEWTON_THIRD * twice
    out = (scale * out).astype(jnp.bfloat16)
    for k in range(NY):
        out_refs[k][...] = out[COLS * k : COLS * (k + 1)].reshape(out_refs[k].shape)


def place_kernel(places, n, aliased, *refs):
    pieces, (out_ref, sems) = refs[:n], refs[n + aliased :]
    y, z = lax.axis_index("y"), lax.axis_index("z")
    side = 1 - 2 * (z & 1)
    copies = []
    for piece, (masks, dz, row) in zip(pieces, places):
        for index, mask in enumerate(masks):
            target = out_ref.at[
                y ^ mask, lax.rem(z + side * dz + NZ, NZ), pl.ds(row, piece.shape[1])
            ]
            copies.append(pltpu.make_async_copy(piece.at[index], target, sems.at[len(copies)]))
            copies[-1].start()
    for copy in copies:
        copy.wait()


def place(out, width, items):
    pieces = near(*(piece for piece, _ in items))
    places = [where for _, where in items]
    n = len(pieces)
    aliased = out is not None
    return pl.pallas_call(
        functools.partial(place_kernel, places, n, int(aliased)),
        out_shape=jax.ShapeDtypeStruct((NY, NZ, COLS, width), jnp.bfloat16),
        in_specs=[VMEM] * n + [ANY] * aliased,
        out_specs=ANY,
        scratch_shapes=[pltpu.SemaphoreType.DMA((sum(len(w[0]) for w in places),))],
        input_output_aliases={n: 0} if aliased else {},
        compiler_params=pltpu.CompilerParams(vmem_limit_bytes=4 << 20),
    )(*pieces, *([out] if aliased else []))


def move(value, axis, to):
    return lax.ppermute(value, axis, to)


def body(x, g, counts):
    width = g.shape[2]

    far_hbm = functools.partial(pltpu.with_memory_space_constraint, memory_space=pltpu.HBM)
    *sides, mine = pl.pallas_call(
        pack_kernel,
        out_shape=[pltpu.VMEM((NZ, COLS, CAP), jnp.bfloat16)] * NY
        + [pltpu.VMEM((NZ, BLK, width), jnp.bfloat16)],
        in_specs=[ANY] * 3,
        out_specs=[VMEM] * (NY + 1),
        scratch_shapes=[
            pltpu.SMEM((1, NY * NZ), jnp.int32),
            pltpu.SemaphoreType.DMA((NY + 2,)),
        ],
        compiler_params=pltpu.CompilerParams(vmem_limit_bytes=2 << 20),
        name="pack",
    )(
        far_hbm(counts),
        far_hbm(x.transpose(0, 2, 1).reshape(NY, NZ, COLS, CAP)),
        far_hbm(g.reshape(NY, NZ, CAP // BLK, BLK, width)),
    )
    sides = [sides[0]] + [move(sides[k], "y", pair(NY, SIDES[k])) for k in range(1, NY)]
    sides = pl.pallas_call(
        join_kernel,
        out_shape=pltpu.VMEM((NZ, NY, COLS, CAP), jnp.bfloat16),
        in_specs=[VMEM] * NY,
        out_specs=VMEM,
        compiler_params=pltpu.CompilerParams(vmem_limit_bytes=1 << 20),
        name="join",
    )(*near(*sides))
    own = lax.all_to_all(mine, "z", 0, 0, tiled=True)
    xz = lax.all_to_all(sides, "z", 0, 0, tiled=True)

    near_1 = move(own, "x", pair(NX, 1))
    near_3 = move(own, "x", pair(NX, 3))
    far_a = move(near_3[: NZ // 2], "x", pair(NX, 1))
    far_b = move(near_1[NZ // 2 :], "x", pair(NX, 3))
    pieces = [own, near_1, near_3, far_a, far_b]
    pieces = pieces + [move(p, "c", pair(NC, 1)) for p in pieces]

    grad = pl.pallas_call(
        grad_kernel,
        out_shape=pltpu.VMEM((NY * COLS, width), jnp.bfloat16),
        in_specs=[VMEM] * 11,
        out_specs=VMEM,
        scratch_shapes=[pltpu.VMEM((NZ, CAP // BLK, BLK, width), jnp.bfloat16)],
        compiler_params=pltpu.CompilerParams(vmem_limit_bytes=12 << 20),
        name="grad",
    )(*near(xz, *pieces))

    mid = NY * COLS // 2
    near_1 = move(grad, "x", pair(NX, 1))
    near_3 = move(grad, "x", pair(NX, 3))
    total = gram_of(grad)
    far_a = move(near_3[:mid], "x", pair(NX, 1))
    far_b = move(near_1[mid:], "x", pair(NX, 3))
    total = total + (gram_of(near_1) + gram_of(near_3))
    other = move(total, "c", pair(NC, 1))
    other_far_a = move(far_a, "c", pair(NC, 1))
    other_far_b = move(far_b, "c", pair(NC, 1))
    total = total + (gram_of(far_a) + gram_of(far_b))

    pieces = pl.pallas_call(
        functools.partial(newton_kernel, math.sqrt(2048)),
        out_shape=[pltpu.VMEM((1, COLS, width), jnp.bfloat16)] * NY,
        in_specs=[VMEM] * 5,
        out_specs=[VMEM] * NY,
        compiler_params=pltpu.CompilerParams(vmem_limit_bytes=32 << 20),
        name="newton",
    )(*near(total, other, other_far_a, other_far_b, grad))

    rows = [pieces[0]] + [move(pieces[k], "y", pair(NY, SIDES[k])) for k in range(1, NY)]
    half = COLS // 2
    items = []
    for ks in CHUNKS:
        piece = jnp.stack([rows[k][0] for k in ks])
        masks = tuple(SIDES[k] for k in ks)
        items.append([(piece, (masks, 0, 0))])
        even, odd = piece, piece
        for n in range(1, 4):
            even, odd = (move(odd, "z", link(NZ, 0)), move(even, "z", link(NZ, 1)))
            items[-1] += [(even, (masks, n, 0)), (odd, (masks, -n, 0))]
        even, odd = (move(odd[:, :half], "z", link(NZ, 0)), move(even[:, half:], "z", link(NZ, 1)))
        items[-1] += [(even, (masks, 4, 0)), (odd, (masks, -4, half))]
    a, b = items
    out = place(None, width, a[:5] + b[:3])
    out = place(out, width, a[5:7] + b[3:5])
    out = place(out, width, a[7:] + b[5:7])
    out = place(out, width, b[7:])
    return out.reshape(NY * NZ, COLS, width)


def solution(mesh):
    fine = Mesh(mesh.devices.reshape(NZ, NY, NX, NC), ("z", "y", "x", "c"))
    return jax.shard_map(
        body,
        mesh=fine,
        in_specs=(P(None, "z", ("y", "x", "c")), P(None, "z", None), P("z", None)),
        out_specs=P(None, ("y", "x", "c"), None),
        check_vma=False,
    )
```

```python
import functools
import math

import jax
import jax.numpy as jnp
from jax import lax
from jax.experimental import pallas as pl
from jax.experimental.pallas import tpu as pltpu
from jax.sharding import Mesh, PartitionSpec as P

BLK = 16
NEWTON_FIRST = 3.4445
NEWTON_SECOND = -4.775
NEWTON_THIRD = 2.0315
EPSILON = 1e-07


NZ, NY, NX, NC = 8, 4, 4, 2
COLS, CAP = 64, 128
SIDES = (0, 1, 3, 2)
CHUNKS = ((0, 1), (2, 3))

VMEM = pl.BlockSpec(memory_space=pltpu.VMEM)
ANY = pl.BlockSpec(memory_space=pl.ANY)


def pair(n, mask):
    return [(i, i ^ mask) for i in range(n)]


def link(n, odd):
    return [(i, (i + (1 if i % 2 == odd else n - 1)) % n) for i in range(n)]


def near(*arrays):
    return [pltpu.with_memory_space_constraint(a, pltpu.VMEM) for a in arrays]


def dot(a, b):
    return jnp.dot(a, b, preferred_element_type=jnp.float32)


def gram_of(rows):
    return lax.dot_general(rows, rows, (((0,), (0,)), ((), ())), preferred_element_type=jnp.float32)


def pack_kernel(count_hbm, x_ref, g_ref, *refs):
    x_outs, g_out, count_ref, sems = refs[:NY], *refs[NY:]
    y = lax.axis_index("y")
    block = NC * lax.axis_index("x") + lax.axis_index("c")
    copies = [
        pltpu.make_async_copy(g_ref.at[y, :, block], g_out, sems.at[NY]),
        pltpu.make_async_copy(count_hbm, count_ref, sems.at[NY + 1]),
    ]
    for k, mask in enumerate(SIDES):
        source = x_ref.at[y ^ mask]
        copies.append(pltpu.make_async_copy(source, x_outs[k], sems.at[k]))
    for copy in copies:
        copy.start()
    for copy in copies:
        copy.wait()
    for plane in range(NZ):

        @pl.when(block >= count_ref[0, NZ * y + plane])
        def _():
            g_out[plane] = jnp.zeros(g_out.shape[1:], g_out.dtype)


def grad_kernel(xt_ref, *refs):
    pieces, out_ref, rows = refs[:-2], refs[-2], refs[-1]
    x, c = lax.axis_index("x"), lax.axis_index("c")
    half = NZ // 2
    for core in range(NC):
        own, near_1, near_3, far_a, far_b = pieces[5 * core : 5 * core + 5]
        for mask, ref, first in (
            (0, own, 0),
            (1, near_1, 0),
            (3, near_3, 0),
            (2, far_a, 0),
            (2, far_b, half),
        ):
            block = NC * (x ^ mask) + (c if core == 0 else 1 - c)
            for r in range(ref.shape[0]):
                rows[first + r, block] = ref[r]
    total = None
    for r in range(0, NZ, 2):
        lhs = jnp.concatenate(
            [xt_ref[r].reshape(NY * COLS, CAP), xt_ref[r + 1].reshape(NY * COLS, CAP)], axis=1
        )
        part = dot(lhs, rows[r : r + 2].reshape(2 * CAP, rows.shape[-1]))
        total = part if total is None else total + part
    out_ref[...] = total.astype(jnp.bfloat16)


def newton_kernel(scale, mine_ref, other_ref, far_a_ref, far_b_ref, grad_ref, *out_refs):
    far = jnp.concatenate([far_a_ref[...], far_b_ref[...]], axis=0)
    raw = mine_ref[...] + other_ref[...] + gram_of(far)
    n = raw.shape[0]
    diagonal = lax.broadcasted_iota(jnp.int32, (n, n), 0) == lax.broadcasted_iota(
        jnp.int32, (n, n), 1
    )
    norm = jnp.sqrt(jnp.sum(jnp.where(diagonal, raw, 0.0), keepdims=True))
    inverse = 1.0 / (norm + EPSILON)
    gram = raw * inverse * inverse
    gram16 = gram.astype(jnp.bfloat16)
    first = (NEWTON_SECOND * gram + NEWTON_THIRD * dot(gram16, gram16)).astype(jnp.bfloat16)
    grad = grad_ref[...]
    current = inverse * (NEWTON_FIRST * grad.astype(jnp.float32) + dot(grad, first))
    half = NEWTON_FIRST * gram + dot(first, gram16)
    gram = NEWTON_FIRST * half + dot(half.astype(jnp.bfloat16), first)
    gram16 = gram.astype(jnp.bfloat16)
    once = dot(current.astype(jnp.bfloat16), gram16)
    twice = dot(once.astype(jnp.bfloat16), gram16)
    out = NEWTON_FIRST * current + NEWTON_SECOND * once + NEWTON_THIRD * twice
    out = (scale * out).astype(jnp.bfloat16)
    for k in range(NY):
        out_refs[k][...] = out[COLS * k : COLS * (k + 1)].reshape(out_refs[k].shape)


def place_kernel(places, n, aliased, *refs):
    pieces, (out_ref, sems) = refs[:n], refs[n + aliased :]
    y, z = lax.axis_index("y"), lax.axis_index("z")
    side = 1 - 2 * (z & 1)
    copies = []
    for piece, (masks, dz, row) in zip(pieces, places):
        for index, mask in enumerate(masks):
            target = out_ref.at[
                y ^ mask, lax.rem(z + side * dz + NZ, NZ), pl.ds(row, piece.shape[1])
            ]
            copies.append(pltpu.make_async_copy(piece.at[index], target, sems.at[len(copies)]))
            copies[-1].start()
    for copy in copies:
        copy.wait()


def place(out, width, items):
    pieces = near(*(piece for piece, _ in items))
    places = [where for _, where in items]
    n = len(pieces)
    aliased = out is not None
    return pl.pallas_call(
        functools.partial(place_kernel, places, n, int(aliased)),
        out_shape=jax.ShapeDtypeStruct((NY, NZ, COLS, width), jnp.bfloat16),
        in_specs=[VMEM] * n + [ANY] * aliased,
        out_specs=ANY,
        scratch_shapes=[pltpu.SemaphoreType.DMA((sum(len(w[0]) for w in places),))],
        input_output_aliases={n: 0} if aliased else {},
        compiler_params=pltpu.CompilerParams(vmem_limit_bytes=4 << 20),
    )(*pieces, *([out] if aliased else []))


def move(value, axis, to):
    return lax.ppermute(value, axis, to)


def body(x, g, counts):
    width = g.shape[2]

    far_hbm = functools.partial(pltpu.with_memory_space_constraint, memory_space=pltpu.HBM)
    *sides, mine = pl.pallas_call(
        pack_kernel,
        out_shape=[pltpu.VMEM((NZ, COLS, CAP), jnp.bfloat16)] * NY
        + [pltpu.VMEM((NZ, BLK, width), jnp.bfloat16)],
        in_specs=[ANY] * 3,
        out_specs=[VMEM] * (NY + 1),
        scratch_shapes=[
            pltpu.SMEM((1, NY * NZ), jnp.int32),
            pltpu.SemaphoreType.DMA((NY + 2,)),
        ],
        compiler_params=pltpu.CompilerParams(vmem_limit_bytes=2 << 20),
        name="pack",
    )(
        far_hbm(counts),
        far_hbm(x.transpose(0, 2, 1).reshape(NY, NZ, COLS, CAP)),
        far_hbm(g.reshape(NY, NZ, CAP // BLK, BLK, width)),
    )
    sides = [sides[0]] + [move(sides[k], "y", pair(NY, SIDES[k])) for k in range(1, NY)]
    sides = jnp.stack(sides, axis=1)
    own = lax.all_to_all(mine, "z", 0, 0, tiled=True)
    xz = lax.all_to_all(sides, "z", 0, 0, tiled=True)

    near_1 = move(own, "x", pair(NX, 1))
    near_3 = move(own, "x", pair(NX, 3))
    far_a = move(near_3[: NZ // 2], "x", pair(NX, 1))
    far_b = move(near_1[NZ // 2 :], "x", pair(NX, 3))
    pieces = [own, near_1, near_3, far_a, far_b]
    pieces = pieces + [move(p, "c", pair(NC, 1)) for p in pieces]

    grad = pl.pallas_call(
        grad_kernel,
        out_shape=pltpu.VMEM((NY * COLS, width), jnp.bfloat16),
        in_specs=[VMEM] * 11,
        out_specs=VMEM,
        scratch_shapes=[pltpu.VMEM((NZ, CAP // BLK, BLK, width), jnp.bfloat16)],
        compiler_params=pltpu.CompilerParams(vmem_limit_bytes=12 << 20),
        name="grad",
    )(*near(xz, *pieces))

    mid = NY * COLS // 2
    near_1 = move(grad, "x", pair(NX, 1))
    near_3 = move(grad, "x", pair(NX, 3))
    total = gram_of(grad)
    far_a = move(near_3[:mid], "x", pair(NX, 1))
    far_b = move(near_1[mid:], "x", pair(NX, 3))
    total = total + (gram_of(near_1) + gram_of(near_3))
    other = move(total, "c", pair(NC, 1))
    other_far_a = move(far_a, "c", pair(NC, 1))
    other_far_b = move(far_b, "c", pair(NC, 1))
    total = total + (gram_of(far_a) + gram_of(far_b))

    pieces = pl.pallas_call(
        functools.partial(newton_kernel, math.sqrt(2048)),
        out_shape=[pltpu.VMEM((1, COLS, width), jnp.bfloat16)] * NY,
        in_specs=[VMEM] * 5,
        out_specs=[VMEM] * NY,
        compiler_params=pltpu.CompilerParams(vmem_limit_bytes=32 << 20),
        name="newton",
    )(*near(total, other, other_far_a, other_far_b, grad))

    rows = [pieces[0]] + [move(pieces[k], "y", pair(NY, SIDES[k])) for k in range(1, NY)]
    half = COLS // 2
    items = []
    for ks in CHUNKS:
        piece = jnp.stack([rows[k][0] for k in ks])
        masks = tuple(SIDES[k] for k in ks)
        items.append([(piece, (masks, 0, 0))])
        even, odd = piece, piece
        for n in range(1, 4):
            even, odd = (move(odd, "z", link(NZ, 0)), move(even, "z", link(NZ, 1)))
            items[-1] += [(even, (masks, n, 0)), (odd, (masks, -n, 0))]
        even, odd = (move(odd[:, :half], "z", link(NZ, 0)), move(even[:, half:], "z", link(NZ, 1)))
        items[-1] += [(even, (masks, 4, 0)), (odd, (masks, -4, half))]
    a, b = items
    out = place(None, width, a[:5] + b[:3])
    out = place(out, width, a[5:7] + b[3:5])
    out = place(out, width, a[7:] + b[5:7])
    out = place(out, width, b[7:])
    return out.reshape(NY * NZ, COLS, width)


def solution(mesh):
    fine = Mesh(mesh.devices.reshape(NZ, NY, NX, NC), ("z", "y", "x", "c"))
    return jax.shard_map(
        body,
        mesh=fine,
        in_specs=(P(None, "z", ("y", "x", "c")), P(None, "z", None), P("z", None)),
        out_specs=P(None, ("y", "x", "c"), None),
        check_vma=False,
    )
```
